512 devices in a mesh: dp: 4 (over x), expert: 8 (over y), etp: 16 (over z, core).
Axes of the slice: x: 4, y: 8, z: 8, core: 2. Of those that a mesh axis runs over, the one named last changes fastest.
Arguments:
- tokens: bfloat16 [4096, 3072], P(('dp', 'expert')), parts along dimension 0, may hold values from -6 to 6
- routes: int32 [4096, 2], P(('dp', 'expert')), parts along dimension 0, may hold values from 0 to 3, all different within a row; in each aligned block of 128 rows (0 to 127, 128 to 255, ...) at most 80 rows name the same one
- route_weight: float32 [4096, 2], P(('dp', 'expert')), parts along dimension 0, may hold values from 0.2 to 1
- w_in: bfloat16 [8, 3072, 4096], P('expert', None, 'etp'), may hold values from -0.109375 to 0.109375
- w_out: bfloat16 [8, 4096, 3072], P('expert', 'etp'), may hold values from -0.0625 to 0.0625
Outputs:
- moe_output: bfloat16 [4096, 3072], P(('dp', 'expert')), parts along dimension 0
The draws below stay inside these ranges and needn't reach their ends.
There are 4 independent parts, one for each index of `dp`. The reference program is written for one: setup_inputs(seed, part) draws one part's arguments, and reference() takes and returns one part's arrays. A program takes and returns all parts, laid end to end along the dimension named above; an argument that names none is the same for every part. Nothing has to cross between parts.
Inputs may be any that keep to these rules, and one draw needn't show every extreme that they name: `routes`: each row names two different experts. Within each aligned block of 128 rows (the rows of one index of the expert axis) no expert is named by more than 80 rows, a bound that some block reaches.
All inputs are finite; a program needn't handle non-finite values.
Results may differ from the reference program's by a relative error of at most 0.018.
Values may be sent and summed in bfloat16 or wider, within the bound.
No kernel may reach another device: no remote copies, remote signals or barrier semaphores. Data moves between devices by JAX's collectives and lax.ppermute only.
A program may use at most 64 MiB of HBM per device.

```python
import math
import jax
import jax.numpy as jnp
import numpy as np
from jax import lax

D = 3072
HID_DEV = 256
TOK_GRP = 128
HALVES = 2
EXPERTS = 4
HIDDEN_SIZE = 8192
CAP = 80
TOKENS = 1024
N_EXPERT = 8
N_ETP = 16


def block_levels(own_key, dims, split, least, top_value):
    factor_of, own = 1.0, jax.random.fold_in(own_key, 6)
    for dim, blocks in split:
        steps = jnp.exp(jax.random.uniform(jax.random.fold_in(own, dim), (blocks,), jnp.float32, least / len(split), top_value / len(split)))
        factor_of = factor_of * jnp.repeat(steps, dims[dim] // blocks).reshape([-1 if axis == dim else 1 for axis in range(len(dims))])
    return factor_of


def shared_out(key, own, number, rows, amount, top, reach, skew):
    sequence = jax.random.permutation(key, amount)
    packed, usual = portions_of(amount, rows * top, reach, skew, True), portions_of(amount, rows * top, reach, skew, False)
    places = jnp.arange(amount)

    def named(lengths, rotation):
        used = int((lengths > 0).sum())
        fixed = max(1, used // 4)
        passed = fixed + (places - fixed + rotation * (used - fixed)) % max(1, amount - fixed)
        return jnp.zeros((amount,), jnp.int32).at[sequence[jnp.where(places < fixed, places, passed)]].set(jnp.asarray(lengths, jnp.int32))

    lengths = jnp.where(number % 4 == 0, named(packed, number // 4), named(usual, number - number // 4 - 1))
    mixed = jax.random.permutation(jax.random.fold_in(own, 3), amount)
    source_of, taker = mixed[0:amount // 2 * 2:2], mixed[1:amount // 2 * 2:2]
    margin = jnp.minimum(lengths[source_of] - 1, reach - lengths[taker]) // 2
    margin = jnp.where((source_of == sequence[0]) | (taker == sequence[0]) | (lengths[taker] == 0), 0, jnp.maximum(margin, 0))
    passed = jax.random.randint(jax.random.fold_in(own, 4), (amount // 2,), 0, 1 << 20) % (margin + 1)
    lengths = lengths.at[source_of].add(-passed).at[taker].add(passed)
    items = jnp.searchsorted(jnp.cumsum(lengths), jnp.arange(rows * top), side="right").astype(jnp.int32)
    listing = items.reshape(top, rows).T
    listing = listing[jax.random.permutation(jax.random.fold_in(own, 1), rows)]
    rotation = jax.random.randint(jax.random.fold_in(own, 2), (rows, 1), 0, top)
    return jnp.take_along_axis(listing, (jnp.arange(top)[None, :] + rotation) % top, axis=1)


def portions_of(count, total, most, slope, full):
    weights = [(1 << 20) // math.isqrt(grade ** slope) + 1 for grade in range(1, count + 1)]
    largest = most if full else min(most, max(-(-total // count), total * weights[0] // sum(weights)))
    least = 1 if total - largest >= count - 1 else 0
    holding, rest = [largest] + [least] * (count - 1), total - largest - least * (count - 1)
    while rest > 0:
        free = [i for i in range(1, count) if holding[i] < largest] or [i for i in range(1, count) if holding[i] < most]
        pool, remaining = sum([weights[i] for i in free]), rest
        for i in free:
            addition = min(most - holding[i], max(1, remaining * weights[i] // pool), rest)
            holding[i] = holding[i] + addition
            rest = rest - addition
    return np.array(holding)


def noise(rng, extent, width, reach, cuts=(), kind=jnp.bfloat16):
    array = width * jax.random.normal(rng, extent, jnp.float32)
    if cuts:
        array = array * block_levels(rng, extent, cuts, -0.22, 0.18)
    return jnp.clip(array, -reach, reach).astype(kind)


def setup_inputs(seed: int = 0, part: int = 0) -> dict:
    seeds = jax.random.split(jax.random.key(seed), 6)
    own_keys = jax.random.split(jax.random.fold_in(seeds[5], part), 6)
    tokens = noise(own_keys[0], (TOKENS, D), 1.0, 6.0, ((0, 8),))
    routes_keys = jax.random.split(jax.random.fold_in(own_keys[1], 1), TOKENS // TOK_GRP)
    routes_turns = jax.random.permutation(jax.random.fold_in(own_keys[1], 3), TOKENS // TOK_GRP)
    routes = jax.vmap(lambda own, number: shared_out(jax.random.fold_in(own_keys[1], 2), own, number, TOK_GRP, EXPERTS, 2, CAP, 2))(routes_keys, routes_turns).reshape((TOKENS, 2))
    route_weight = jnp.clip(0.2 + 0.8 * jax.random.uniform(own_keys[2], (TOKENS, 2), jnp.float32) ** block_levels(own_keys[2], (TOKENS, 2), ((0, 8),), -0.2, 0.2), 0.2, 1.0)
    w_in = noise(seeds[3], (N_EXPERT, D, HID_DEV * N_ETP), D ** -0.5, 0.109375, ((0, 8), (2, 16)))
    w_out = noise(seeds[4], (N_EXPERT, HID_DEV * N_ETP, D), HIDDEN_SIZE ** -0.5, 0.0625, ((0, 8), (1, 16)))
    return dict(tokens=tokens, routes=routes, route_weight=route_weight, w_in=w_in, w_out=w_out)


def shard_terms(hidden, w_down):
    hidden_groups = jnp.transpose(hidden.reshape(TOKENS, N_ETP, HID_DEV), (1, 0, 2))
    weight_groups = w_down.reshape(N_ETP, HID_DEV, D)

    def shard_step(running, pair):
        term = jnp.dot(pair[0], pair[1], preferred_element_type=jnp.float32)
        rounded = lax.optimization_barrier(term.astype(jnp.bfloat16))
        return running + rounded.astype(jnp.float32), None

    initial = jnp.zeros((TOKENS, D), jnp.float32)
    running, _ = lax.scan(shard_step, initial, (hidden_groups, weight_groups))
    return running


def reference(tokens, routes, route_weight, w_in, w_out):
    def per_index(index):
        projected = jnp.dot(tokens, w_in[index], preferred_element_type=jnp.float32)
        hidden = jax.nn.silu(projected).astype(jnp.bfloat16)
        return shard_terms(hidden, w_out[index])

    blocks = lax.map(per_index, jnp.arange(N_EXPERT, dtype=jnp.int32))
    per_expert = jnp.sum(blocks.reshape(EXPERTS, HALVES, TOKENS, D), axis=1)
    row_index = jnp.arange(TOKENS, dtype=jnp.int32)
    combined = jnp.zeros((TOKENS, D), jnp.float32)
    for column in range(2):
        picked = per_expert[routes[:, column], row_index]
        combined = combined + route_weight[:, column][:, None] * picked
    return combined.astype(jnp.bfloat16)
```

```python
import jax
import jax.numpy as jnp
from jax import lax
from jax.experimental import pallas as pl
from jax.experimental.pallas import tpu as pltpu
from jax.sharding import Mesh
from jax.sharding import PartitionSpec as P

N_EXPERTS = 4
F32 = jnp.float32
BF16 = jnp.bfloat16
I32 = jnp.int32


def slots_of(routes_t):
    tok = routes_t.shape[1]
    first, second = routes_t[0:1, :], routes_t[1:2, :]
    named = [((first == e) | (second == e)) for e in range(N_EXPERTS)]
    stacked = jnp.concatenate(
        [jnp.where(n, 1.0, 0.0) for n in named] + [jnp.zeros((4, tok), F32)], axis=0
    )
    earlier = lax.broadcasted_iota(I32, (tok, tok), 0) < lax.broadcasted_iota(I32, (tok, tok), 1)
    counts = jnp.dot(
        stacked.astype(BF16),
        jnp.where(earlier, 1.0, 0.0).astype(BF16),
        preferred_element_type=F32,
    )
    return named, [counts[e : e + 1, :].astype(I32) for e in range(N_EXPERTS)]


def pack_kernel(core_ref, routes_ref, tokens_ref, out_ref):
    half_cap = out_ref.shape[1]
    tok = tokens_ref.shape[0]
    named, place = slots_of(routes_ref[...])
    tokens = tokens_ref[...]
    slot = lax.broadcasted_iota(I32, (half_cap, tok), 0) + core_ref[0] * half_cap
    for e in range(N_EXPERTS):
        chosen = jnp.where(named[e] & (place[e] == slot), 1.0, 0.0).astype(BF16)
        rows = jnp.dot(chosen, tokens, preferred_element_type=F32).astype(BF16)
        out_ref[2 * e] = rows
        out_ref[2 * e + 1] = rows


def ffn_kernel(x_ref, wi_a_ref, wi_b_ref, wo_a_ref, wo_b_ref, out_ref, acc_a, acc_b, hid_a, hid_b, *, steps):
    step = pl.program_id(0)

    @pl.when(step == 0)
    def _():
        acc_a[...] = jnp.zeros_like(acc_a)
        acc_b[...] = jnp.zeros_like(acc_b)

    @pl.when(step < steps)
    def _():
        x = x_ref[...]
        acc_a[...] += jnp.dot(x, wi_a_ref[0], preferred_element_type=F32)
        acc_b[...] += jnp.dot(x, wi_b_ref[0], preferred_element_type=F32)

    @pl.when(step == steps - 1)
    def _():
        a = acc_a[...]
        b = acc_b[...]
        hid_a[...] = (a / (1.0 + jnp.exp(-a))).astype(BF16)
        hid_b[...] = (b / (1.0 + jnp.exp(-b))).astype(BF16)

    @pl.when(step >= steps)
    def _():
        term = jnp.dot(hid_a[...], wo_a_ref[0], preferred_element_type=F32)
        term += jnp.dot(hid_b[...], wo_b_ref[0], preferred_element_type=F32)
        width = out_ref.shape[2]
        for k in range(out_ref.shape[0]):
            out_ref[k] = term[:, k * width : (k + 1) * width].astype(BF16)


def ffn(x, wi_a, wi_b, wo_a, wo_b, n_z):
    rows, width = x.shape
    hidden = wi_a.shape[2]
    steps = 4
    wk = width // steps
    k_of = lambda s: jnp.minimum(s, steps - 1)
    c_of = lambda s: jnp.maximum(s - steps, 0)
    return pl.pallas_call(
        lambda *refs: ffn_kernel(*refs, steps=steps),
        grid=(2 * steps,),
        in_specs=[
            pl.BlockSpec((rows, wk), lambda s: (0, k_of(s))),
            pl.BlockSpec((1, wk, hidden), lambda s: (0, k_of(s), 0)),
            pl.BlockSpec((1, wk, hidden), lambda s: (0, k_of(s), 0)),
            pl.BlockSpec((1, hidden, wk), lambda s: (0, 0, c_of(s))),
            pl.BlockSpec((1, hidden, wk), lambda s: (0, 0, c_of(s))),
        ],
        out_specs=pl.BlockSpec((n_z // steps, rows, width // n_z), lambda s: (c_of(s), 0, 0)),
        out_shape=jax.ShapeDtypeStruct((n_z, rows, width // n_z), BF16),
        scratch_shapes=[pltpu.VMEM((rows, hidden), F32)] * 2 + [pltpu.VMEM((rows, hidden), BF16)] * 2,
        name="ffn",
    )(x, wi_a, wi_b, wo_a, wo_b)


def combine_kernel(core_ref, routes_ref, weight_ref, terms_ref, keep_ref, send_ref, part_ref):
    n_z, n_y, half_cap, width = terms_ref.shape
    tok = routes_ref.shape[1]
    named, place = slots_of(routes_ref[...])
    routes = routes_ref[...]
    weight = weight_ref[...]
    core = core_ref[0]
    slot = lax.broadcasted_iota(I32, (half_cap, tok), 0) + core * half_cap
    scaled, summed = [], []
    for e in range(N_EXPERTS):
        of_e = jnp.where(routes[0:1, :] == e, weight[0:1, :], weight[1:2, :])
        scaled.append(jnp.where(named[e] & (place[e] == slot), of_e, 0.0))
        total = jnp.zeros((half_cap, width), F32)
        for z in range(n_z):
            total += terms_ref[z, 2 * e].astype(F32) + terms_ref[z, 2 * e + 1].astype(F32)
        summed.append(total)
    part_ref[...] = lax.dot_general(
        jnp.concatenate(scaled, axis=0),
        jnp.concatenate(summed, axis=0),
        (((0,), (0,)), ((), ())),
        precision=lax.Precision.HIGHEST,
        preferred_element_type=F32,
    )
    half = tok // 2
    keep_ref[...] = part_ref[pl.ds(pl.multiple_of(core * half, half), half), :]
    send_ref[...] = part_ref[pl.ds(pl.multiple_of((1 - core) * half, half), half), :]


SMEM = pl.BlockSpec(memory_space=pltpu.SMEM)
VMEM = pl.BlockSpec(memory_space=pltpu.VMEM)


def on_device(tokens, routes, route_weight, w_in, w_out):
    n_y = lax.axis_size("expert")
    n_z = lax.axis_size("z")
    tok, width = tokens.shape
    half_cap = 40
    core = lax.axis_index("core").astype(I32).reshape(1)
    swap = [(0, 1), (1, 0)]
    w_in_other = lax.ppermute(w_in, "core", swap)
    w_out_other = lax.ppermute(w_out, "core", swap)
    routes_t = routes.T
    weight_t = route_weight.T

    packed = pl.pallas_call(
        pack_kernel,
        in_specs=[SMEM, VMEM, VMEM],
        out_specs=VMEM,
        out_shape=jax.ShapeDtypeStruct((n_y, half_cap, width), BF16),
        name="pack",
    )(core, routes_t, tokens)
    arrived = lax.all_to_all(packed, "expert", split_axis=0, concat_axis=0, tiled=True)

    terms = ffn(arrived.reshape(n_y * half_cap, width), w_in, w_in_other, w_out, w_out_other, n_z)

    home = lax.all_to_all(
        terms.reshape(n_z * n_y, half_cap, width // n_z),
        ("z", "expert"),
        split_axis=0,
        concat_axis=0,
        tiled=True,
    ).reshape(n_z, n_y, half_cap, width // n_z)

    half = jax.ShapeDtypeStruct((tok // 2, width // n_z), F32)
    keep, send = pl.pallas_call(
        combine_kernel,
        in_specs=[SMEM, VMEM, VMEM, VMEM],
        out_specs=(VMEM, VMEM),
        out_shape=(half, half),
        scratch_shapes=[pltpu.VMEM((tok, width // n_z), F32)],
        name="combine",
    )(core, routes_t, weight_t, home)
    mine = (keep + lax.ppermute(send, "core", swap)).astype(BF16)
    every = lax.all_gather(mine, ("z", "core"), axis=0, tiled=False)
    every = every.reshape(n_z, 2, tok // 2, width // n_z)
    return every.transpose(1, 2, 0, 3).reshape(tok, width)


def solution(mesh):
    n_dp, n_y, n_etp = (mesh.shape[a] for a in ("dp", "expert", "etp"))
    by_core = Mesh(mesh.devices.reshape(n_dp, n_y, n_etp // 2, 2), ("dp", "expert", "z", "core"))
    rows = P(("dp", "expert"), None)
    return jax.shard_map(
        on_device,
        mesh=by_core,
        in_specs=(rows, rows, rows, P("expert", None, ("z", "core")), P("expert", ("z", "core"), None)),
        out_specs=rows,
        check_vma=False,
    )
```

```python
import jax
import jax.numpy as jnp
from jax import lax
from jax.experimental import pallas as pl
from jax.experimental.pallas import tpu as pltpu
from jax.sharding import Mesh
from jax.sharding import PartitionSpec as P

N_EXPERTS = 4
F32 = jnp.float32
BF16 = jnp.bfloat16
I32 = jnp.int32


def slots_of(routes_t):
    tok = routes_t.shape[1]
    first, second = routes_t[0:1, :], routes_t[1:2, :]
    named = [((first == e) | (second == e)) for e in range(N_EXPERTS)]
    stacked = jnp.concatenate(
        [jnp.where(n, 1.0, 0.0) for n in named] + [jnp.zeros((4, tok), F32)], axis=0
    )
    earlier = lax.broadcasted_iota(I32, (tok, tok), 0) < lax.broadcasted_iota(I32, (tok, tok), 1)
    counts = jnp.dot(
        stacked.astype(BF16),
        jnp.where(earlier, 1.0, 0.0).astype(BF16),
        preferred_element_type=F32,
    )
    return named, [counts[e : e + 1, :].astype(I32) for e in range(N_EXPERTS)]


def pack_kernel(ids_ref, routes_ref, tokens_ref, out_ref):
    half_cap, width = out_ref.shape[1:]
    tok = tokens_ref.shape[0]
    named, place = slots_of(routes_ref[...])
    tokens = tokens_ref[:, pl.ds(pl.multiple_of(ids_ref[1] * width, width), width)]
    slot = lax.broadcasted_iota(I32, (half_cap, tok), 0) + ids_ref[0] * half_cap
    for e in range(N_EXPERTS):
        chosen = jnp.where(named[e] & (place[e] == slot), 1.0, 0.0).astype(BF16)
        rows = jnp.dot(chosen, tokens, preferred_element_type=F32).astype(BF16)
        out_ref[2 * e] = rows
        out_ref[2 * e + 1] = rows


def rows_of(w_ref, part, size):
    return w_ref[0, pl.ds(pl.multiple_of(part * size, size), size), :]


def cols_of(w_ref, block, size):
    return w_ref[0, :, pl.ds(pl.multiple_of(block * size, size), size)]


def own_half_kernel(ids_ref, x_ref, wi_a_ref, wi_b_ref, acc_a, acc_b):
    x = x_ref[...]
    size = x.shape[1]
    acc_a[...] = jnp.dot(x, rows_of(wi_a_ref, ids_ref[1], size), preferred_element_type=F32)
    acc_b[...] = jnp.dot(x, rows_of(wi_b_ref, ids_ref[1], size), preferred_element_type=F32)


def other_half_kernel(ids_ref, x_ref, wi_a_ref, wi_b_ref, acc_a, acc_b, wo_a_ref, wo_b_ref, hid_a, hid_b, send_ref):
    x = x_ref[...]
    size = x.shape[1]
    for wi_ref, acc, hid in ((wi_a_ref, acc_a, hid_a), (wi_b_ref, acc_b, hid_b)):
        v = acc[...] + jnp.dot(x, rows_of(wi_ref, 1 - ids_ref[1], size), preferred_element_type=F32)
        hid[...] = (v / (1.0 + jnp.exp(-v))).astype(BF16)
    columns(1 - ids_ref[1], hid_a, hid_b, wo_a_ref, wo_b_ref, send_ref)


def keep_kernel(ids_ref, hid_a, hid_b, wo_a_ref, wo_b_ref, keep_ref):
    columns(ids_ref[1], hid_a, hid_b, wo_a_ref, wo_b_ref, keep_ref)


def columns(parity, hid_a, hid_b, wo_a_ref, wo_b_ref, out_ref):
    size = out_ref.shape[2]
    for k in range(out_ref.shape[0]):
        term = jnp.dot(hid_a[...], cols_of(wo_a_ref, 2 * k + parity, size), preferred_element_type=F32)
        term += jnp.dot(hid_b[...], cols_of(wo_b_ref, 2 * k + parity, size), preferred_element_type=F32)
        out_ref[k] = term.astype(out_ref.dtype)


def combine_kernel(core_ref, routes_ref, weight_ref, terms_ref, keep_ref, send_ref, part_ref):
    n_z, n_y, half_cap, width = terms_ref.shape
    tok = routes_ref.shape[1]
    named, place = slots_of(routes_ref[...])
    routes = routes_ref[...]
    weight = weight_ref[...]
    core = core_ref[0]
    slot = lax.broadcasted_iota(I32, (half_cap, tok), 0) + core * half_cap
    scaled, summed = [], []
    for e in range(N_EXPERTS):
        of_e = jnp.where(routes[0:1, :] == e, weight[0:1, :], weight[1:2, :])
        scaled.append(jnp.where(named[e] & (place[e] == slot), of_e, 0.0))
        total = jnp.zeros((half_cap, width), F32)
        for z in range(n_z):
            total += terms_ref[z, 2 * e].astype(F32) + terms_ref[z, 2 * e + 1].astype(F32)
        summed.append(total)
    part_ref[...] = lax.dot_general(
        jnp.concatenate(scaled, axis=0),
        jnp.concatenate(summed, axis=0),
        (((0,), (0,)), ((), ())),
        precision=lax.Precision.HIGHEST,
        preferred_element_type=F32,
    )
    half = tok // 2
    keep_ref[...] = part_ref[pl.ds(pl.multiple_of(core * half, half), half), :]
    send_ref[...] = part_ref[pl.ds(pl.multiple_of((1 - core) * half, half), half), :]


SMEM = pl.BlockSpec(memory_space=pltpu.SMEM)
VMEM = pl.BlockSpec(memory_space=pltpu.VMEM)


def call(kernel, name, out_shape, ids, *operands, scratch=()):
    several = isinstance(out_shape, tuple)
    return pl.pallas_call(
        kernel,
        in_specs=[SMEM] + [VMEM] * len(operands),
        out_specs=(VMEM,) * len(out_shape) if several else VMEM,
        out_shape=out_shape,
        scratch_shapes=list(scratch),
        name=name,
    )(ids, *operands)


def on_device(tokens, routes, route_weight, w_in, w_out):
    n_y = lax.axis_size("expert")
    n_h = lax.axis_size("zh")
    n_z = 2 * n_h
    tok, width = tokens.shape
    hidden = w_in.shape[2]
    half_cap = 40
    rows = n_y * half_cap
    col = width // n_z
    shape = jax.ShapeDtypeStruct
    z_axes = ("zh", "zl", "core")
    ids = jnp.stack([lax.axis_index("core"), lax.axis_index("zl")]).astype(I32)
    swap = [(0, 1), (1, 0)]
    onward = [(2 * z + c, 2 * ((z + 1 - 2 * c) % n_z) + c) for z in range(n_z) for c in range(2)]
    wi_b = lax.ppermute(w_in, "core", swap)
    wo_b = lax.ppermute(w_out, "core", swap)
    routes_t = routes.T
    weight_t = route_weight.T

    packed = call(pack_kernel, "pack", shape((n_y, half_cap, width // 2), BF16), ids, routes_t, tokens)
    mine = lax.all_to_all(packed, "expert", split_axis=0, concat_axis=0, tiled=True).reshape(rows, width // 2)
    theirs = lax.ppermute(mine, z_axes, onward)

    acc = shape((rows, hidden), F32)
    acc_a, acc_b = call(own_half_kernel, "own_half", (acc, acc), ids, mine, w_in, wi_b)
    hid = shape((rows, hidden), BF16)
    hid_a, hid_b, send = call(
        other_half_kernel,
        "other_half",
        (hid, hid, shape((n_h, rows, col), BF16)),
        ids,
        theirs,
        w_in,
        wi_b,
        acc_a,
        acc_b,
        w_out,
        wo_b,
    )
    got = lax.ppermute(send, z_axes, onward)
    keep = call(keep_kernel, "keep", shape((n_h, rows, col), F32), ids, hid_a, hid_b, w_out, wo_b)
    terms = (keep + got.astype(F32)).astype(BF16)

    home = lax.all_to_all(
        terms.reshape(n_h * n_y, half_cap, col), ("zh", "expert"), split_axis=0, concat_axis=0, tiled=True
    ).reshape(n_h, n_y, half_cap, col)

    half = shape((tok // 2, col), F32)
    keep, send = call(
        combine_kernel,
        "combine",
        (half, half),
        ids,
        routes_t,
        weight_t,
        home,
        scratch=[pltpu.VMEM((tok, col), F32)],
    )
    part = (keep + lax.ppermute(send, "core", swap)).astype(BF16)
    every = lax.all_gather(part, z_axes, axis=0, tiled=False)
    return every.reshape(n_z, 2, tok // 2, col).transpose(1, 2, 0, 3).reshape(tok, width)


def solution(mesh):
    n_dp, n_y, n_etp = (mesh.shape[a] for a in ("dp", "expert", "etp"))
    by_core = Mesh(mesh.devices.reshape(n_dp, n_y, n_etp // 4, 2, 2), ("dp", "expert", "zh", "zl", "core"))
    rows = P(("dp", "expert"), None)
    etp = ("zh", "zl", "core")
    return jax.shard_map(
        on_device,
        mesh=by_core,
        in_specs=(rows, rows, rows, P("expert", None, etp), P("expert", etp, None)),
        out_specs=rows,
        check_vma=False,
    )
```
